256 devices in a mesh: row: 32 (over y, z), col: 8 (over x, core).
Axes of the slice: x: 4, y: 4, z: 8, core: 2. Of those that a mesh axis runs over, the one named last changes fastest.
Arguments:
- lower: float32 [6, 2048, 2048], P(None, 'row', 'col'), may hold values from -0.046875 to 0.046875
- dinv: float32 [4, 2048, 2048], P(None, 'row', 'col'), as said below
- kcols: float32 [4, 2048, 2048], P(None, 'row', 'col'), may hold values from -6 to 6
- prior: float32 [2048], P('col'), may hold values from 3 to 5
Outputs:
- solved_columns: float32 [4, 2048, 2048], P(None, 'row', 'col')
- variance: float32 [2048], P('col')
The draws below stay inside these ranges and needn't reach their ends.
Inputs may be any that keep to these rules, and one draw needn't show every extreme that they name: Each block of dinv is lower triangular with a positive diagonal.
All inputs are finite; a program needn't handle non-finite values.
Results may differ from the reference program's by a relative error of at most 0.0001.
Values sent between devices are 32-bit elements; how exact they have to be, the bound alone decides.
A program may use at most 64 MiB of HBM per device.

```python
import jax
import jax.numpy as jnp
from jax import lax

PANEL = 2048
STEPS = 4
CAND = 2048
PAIRS = 6
OBS = 8192


def draw_dinv(key, part):
    shape = (STEPS, PANEL, PANEL)
    noise_key = jax.random.fold_in(key, 11)
    diag_key = jax.random.fold_in(key, 23)
    noise = jax.random.normal(noise_key, shape, jnp.float32)
    diag_vals = jax.random.uniform(diag_key, shape, jnp.float32, 0.8, 1.2)
    rows_idx = jax.lax.broadcasted_iota(jnp.int32, shape, 1)
    cols_idx = jax.lax.broadcasted_iota(jnp.int32, shape, 2)
    below = (rows_idx > cols_idx).astype(jnp.float32)
    on_diag = (rows_idx == cols_idx).astype(jnp.float32)
    return below * noise * (0.5 / PANEL ** 0.5) + on_diag * diag_vals


def shard_levels(stream_key, dims, pieces, least, top_value):
    loudness, own = 1.0, jax.random.fold_in(stream_key, 6)
    for dim, blocks in pieces:
        steps = jnp.exp(jax.random.uniform(jax.random.fold_in(own, dim), (blocks,), jnp.float32, least / len(pieces), top_value / len(pieces)))
        loudness = loudness * jnp.repeat(steps, dims[dim] // blocks).reshape([-1 if axis == dim else 1 for axis in range(len(dims))])
    return loudness


def normal_values(own_key, dims, spread, bound, shards=(), kind=jnp.bfloat16):
    array = spread * jax.random.normal(own_key, dims, jnp.float32)
    if shards:
        array = array * shard_levels(own_key, dims, shards, -0.22, 0.18)
    return jnp.clip(array, -bound, bound).astype(kind)


def setup_inputs(seed: int = 0) -> dict:
    key_list = jax.random.split(jax.random.key(seed), 5)
    lower = normal_values(key_list[0], (PAIRS, PANEL, PANEL), (8 * PANEL) ** -0.5, 0.046875, ((1, 32), (2, 8)), jnp.float32)
    dinv = draw_dinv(jax.random.fold_in(key_list[4], 71), 0)
    kcols = normal_values(key_list[2], (STEPS, PANEL, CAND), 1.0, 6.0, ((1, 32), (2, 8)), jnp.float32)
    prior = jnp.clip(3.0 + 2.0 * jax.random.uniform(key_list[3], (CAND,), jnp.float32) ** shard_levels(key_list[3], (CAND,), ((0, 8),), -0.2, 0.2), 3.0, 5.0)
    return {"lower": lower, "dinv": dinv, "kcols": kcols, "prior": prior}


def reference(lower, dinv, kcols, prior):
    solved = []
    for segment_now in range(STEPS):
        residual = kcols[segment_now]
        for earlier in range(segment_now):
            residual = residual - jnp.dot(lower[segment_now * (segment_now - 1) // 2 + earlier], solved[earlier], precision=lax.Precision.HIGHEST, preferred_element_type=jnp.float32)
        solved.append(jnp.dot(dinv[segment_now], residual, precision=lax.Precision.HIGHEST, preferred_element_type=jnp.float32))
    solution = jnp.stack(solved)
    variance = prior - jnp.sum(solution * solution, axis=(0, 1)) / OBS
    return solution, variance
```

```python
import functools

import jax
import jax.numpy as jnp
from jax import lax
from jax.experimental import pallas as pl
from jax.experimental.pallas import tpu as pltpu
from jax.sharding import PartitionSpec as P

OBS = 8192
MESH = pl.DeviceIdType.MESH
F32 = jnp.float32
BF16 = jnp.bfloat16


GROUPS = ((6, 1), (0, 1), (7, 1), (1, 2), (8, 1), (3, 3), (9, 1))


def kernel(
    X,
    lower_ref,
    dinv_ref,
    kcols_ref,
    prior_ref,
    out_ref,
    var_ref,
    G,
    HL,
    W,
    KB,
    XG,
    PB,
    RR,
    PE,
    VB,
    VX,
    VN,
    ring_s,
    ring_r,
    sib_s,
    sib_r,
    own_r,
    swap_s,
    gat_s,
    gat_r,
    red_s,
    red_r,
    k_s,
    k_r,
    out_s,
    out_r,
    vx_s,
    vx_r,
    vn_s,
    vn_r,
):
    Y, Z = X, 2 * X
    H = Z // 2
    row, col = lax.axis_index("row"), lax.axis_index("col")
    y, z = row // Z, lax.rem(row, Z)
    x, k = col // 2, lax.rem(col, 2)
    h = kcols_ref.shape[1]
    q = 2 * h
    w = kcols_ref.shape[2] // 2

    def dev(dx, dy, dz, dk):
        return (dy * Z + dz, dx * 2 + dk)

    def up(v, d, m):
        return lax.rem(v + d, m)

    pending = []

    class Copy:
        def __init__(self, src, dst, ssem, rsem, target, me=None):
            self.me = me
            self.remote = pltpu.make_async_remote_copy(
                src_ref=src, dst_ref=dst, send_sem=ssem, recv_sem=rsem, device_id=target, device_id_type=MESH
            )
            self.local = None if me is None else pltpu.make_async_copy(src, dst, rsem)

        def start(self):
            pending.append(self)
            if self.me is None:
                self.remote.start()
            else:
                pl.when(self.me)(self.local.start)
                pl.when(jnp.logical_not(self.me))(self.remote.start)

        def wait_send(self):
            if self.me is None:
                self.remote.wait_send()
            else:
                pl.when(jnp.logical_not(self.me))(self.remote.wait_send)

    def arrived(dst, rsem):
        pltpu.make_async_copy(dst, dst, rsem).wait()

    zu, zd = up(z, 1, Z), up(z, Z - 1, Z)
    above, below = dev(x, y, zu, k), dev(x, y, zd, k)
    sibling = dev(x, y, z, 1 - k)
    partner = dev(y, x, z, k)
    swaps_self = x == y
    xpeer = [None] + [dev(up(x, d, X), y, z, k) for d in range(1, X)]
    ypeer = [None] + [dev(x, up(y, d, Y), z, k) for d in range(1, Y)]
    k_to = [dev(y, z // 2, 2 * x + k, c) for c in range(2)]
    k_to_self = [(x == y) & (y == z // 2) & (z == 2 * x + k) & (k == c) for c in range(2)]
    k_from = [dev(z // 2, x, 2 * y + b, lax.rem(z, 2)) for b in range(2)]
    k_from_self = [(x == z // 2) & (y == x) & (z == 2 * y + b) & (k == lax.rem(z, 2)) for b in range(2)]
    o_to = [[dev(z // 2, yy, 2 * x + b, lax.rem(z, 2)) for b in range(2)] for yy in range(Y)]
    o_to_self = [
        [(x == z // 2) & (y == yy) & (z == 2 * x + b) & (k == lax.rem(z, 2)) for b in range(2)] for yy in range(Y)
    ]
    o_from = [[dev(z // 2, yy, 2 * x + k, c) for c in range(2)] for yy in range(Y)]
    o_from_self = [[(x == z // 2) & (y == yy) & (z == 2 * x + k) & (k == c) for c in range(2)] for yy in range(Y)]

    barrier = pltpu.get_barrier_semaphore()

    def greet(target, me=None):
        def far():
            pl.semaphore_signal(barrier, inc=1, device_id=target, device_id_type=MESH)

        if me is None:
            far()
        else:
            pl.when(jnp.logical_not(me))(far)

    for b in range(2):
        greet(k_from[b], k_from_self[b])
    for yy in range(Y):
        for c in range(2):
            greet(o_from[yy][c], o_from_self[yy][c])
    greet(partner, swaps_self)
    for d in range(1, X):
        greet(xpeer[d])
        greet(ypeer[d])
    greet(above)
    greet(below)
    greet(sibling)
    count = 2 * X + 1
    for me in k_to_self + [swaps_self] + [v for pair in o_to_self for v in pair]:
        count = count + jnp.where(me, 0, 1)
    own = pltpu.make_async_copy(dinv_ref, G.at[pl.ds(6, 4), k, z], own_r.at[0])
    own.start()
    pl.semaphore_wait(barrier, count)

    def piece(g, zz, kk):
        b0, nb = GROUPS[g]
        return G.at[pl.ds(b0, nb), kk, zz]

    def steps(g):
        return (H, Z - 1 - H) if g % 2 == 0 else (Z - 1 - H, H)

    def ring_send(g, upward, j):
        at = up(z, Z - j + 1, Z) if upward else up(z, j - 1, Z)
        lane = 0 if upward else 1
        Copy(
            piece(g, at, k),
            piece(g, at, k),
            ring_s.at[g, lane, j],
            ring_r.at[g, lane, j],
            above if upward else below,
        ).start()

    def sib_send(g, lane, j):
        at = up(z, Z - j, Z) if lane == 0 else up(z, j, Z)
        Copy(piece(g, at, k), piece(g, at, k), sib_s.at[g, lane, j], sib_r.at[g, lane, j], sibling).start()

    def relay(g, j):
        cu, cd = steps(g)
        if j == 1:
            if g % 2 == 1:
                arrived(piece(g, z, k), own_r.at[1 + g // 2])
            ring_send(g, True, 1)
            ring_send(g, False, 1)
            sib_send(g, 0, 0)
            return
        for lane, limit in ((0, cu), (1, cd)):
            if j - 1 <= limit:
                at = up(z, Z - j + 1, Z) if lane == 0 else up(z, j - 1, Z)
                arrived(piece(g, at, k), ring_r.at[g, lane, j - 1])
                if j <= limit:
                    ring_send(g, lane == 0, j)
                sib_send(g, lane, j - 1)

    def split(b):
        for kk in range(2):
            for j in range(X):
                block = jnp.concatenate([G[b, kk, 2 * j], G[b, kk, 2 * j + 1]], axis=0)
                hi = block.astype(BF16)
                HL[b, kk, j, pl.ds(0, q)] = hi
                HL[b, kk, j, pl.ds(q, q)] = (block - hi.astype(F32)).astype(BF16)

    def finish(g):
        cu, cd = steps(g)
        arrived(piece(g, z, 1 - k), sib_r.at[g, 0, 0])
        for lane, limit in ((0, cu), (1, cd)):
            for j in range(1, limit + 1):
                at = up(z, Z - j, Z) if lane == 0 else up(z, j, Z)
                arrived(piece(g, at, 1 - k), sib_r.at[g, lane, j])
        b0, nb = GROUPS[g]
        for b in range(b0, b0 + nb):
            split(b)

    own.wait()
    relay(0, 1)
    for part, (s0, ns) in enumerate(((0, 1), (1, 3))):
        for c in range(2):
            Copy(
                kcols_ref.at[pl.ds(s0, ns), :, pl.ds(c * w, w)],
                KB.at[pl.ds(s0, ns), lax.rem(z, 2)],
                k_s.at[part, c],
                k_r.at[part, lax.rem(z, 2)],
                k_to[c],
                k_to_self[c],
            ).start()
        if part == 0:
            for i, g in enumerate((1, 3, 5)):
                b0, nb = GROUPS[g]
                Copy(
                    lower_ref.at[pl.ds(b0, nb)],
                    piece(g, z, k),
                    swap_s.at[i],
                    own_r.at[1 + i],
                    partner,
                    swaps_self,
                ).start()

    def gather_start(i):
        n_at, peers = (y, ypeer) if i % 2 == 0 else (x, xpeer)
        for d in (2, 1, 3) if X == 4 else range(1, X):
            Copy(XG.at[i, n_at], XG.at[i, n_at], gat_s.at[i, d], gat_r.at[i, d], peers[d]).start()

    def gather_wait(i):
        n_at = y if i % 2 == 0 else x
        for d in range(1, X):
            arrived(XG.at[i, up(n_at, X - d, X)], gat_r.at[i, d])
        full = jnp.concatenate([XG[i, p] for p in range(X)], axis=0)
        hi = full.astype(BF16)
        lo = (full - hi.astype(F32)).astype(BF16)
        both = jnp.concatenate([hi, lo], axis=1)
        half = both.shape[0] // 2
        W[i, 0] = both[:half]
        W[i, 1] = both[half:]

    def product(i, b, j):
        res = jnp.dot(HL[b, 0, j], W[i, 0], preferred_element_type=F32)
        res += jnp.dot(HL[b, 1, j], W[i, 1], preferred_element_type=F32)
        return (res[:q, :w] + res[q:, w:]) + (res[:q, w:] + res[q:, :w])

    def reduce_start(i, blocks, early=None):
        n_at, peers = (x, xpeer) if i % 2 == 0 else (y, ypeer)
        for d in (2, 1, 3, 0) if X == 4 else list(range(1, X)) + [0]:
            j = up(n_at, d, X)
            total = None if early is None else PE[early, j]
            for src, b in blocks:
                term = product(src, b, j)
                total = term if total is None else total + term
            PB[i, d] = total
            if d:
                Copy(PB.at[i, d], RR.at[i, d], red_s.at[i, d], red_r.at[i, d], peers[d]).start()

    def early(slot, blocks):
        for j in range(X):
            total = None
            for src, b in blocks:
                term = product(src, b, j)
                total = term if total is None else total + term
            PE[slot, j] = total

    def reduce_wait(i):
        total = PB[i, 0]
        for d in range(1, X):
            arrived(RR.at[i, d], red_r.at[i, d])
            total = total + RR[i, d]
        return total

    def emit(s, solved, squares):
        src = XG.at[2 * s + 1, x] if s < 3 else PB.at[6, 0]
        for b in range(2):
            me = (x == z // 2) & (z == 2 * x + b) & (k == lax.rem(z, 2))
            Copy(
                src.at[pl.ds(b * h, h)],
                out_ref.at[s, :, pl.ds(pl.multiple_of(k * w, w), w)],
                out_s.at[s, b],
                out_r.at[s, k],
                dev(z // 2, y, 2 * x + b, lax.rem(z, 2)),
                me,
            ).start()
        part = jnp.sum(solved * solved, axis=0, keepdims=True)
        return part if squares is None else squares + part

    def step_in(s):
        if s:
            if s == 1:
                for b in range(2):
                    arrived(KB.at[pl.ds(1, 3), b], k_r.at[1, b])
            total = reduce_wait(2 * s - 1)
            XG[2 * s, y] = jnp.concatenate([KB[s, 0], KB[s, 1]], axis=0) - total
        else:
            for b in range(2):
                arrived(KB.at[pl.ds(0, 1), b], k_r.at[0, b])
            XG[0, y] = jnp.concatenate([KB[0, 0], KB[0, 1]], axis=0)
        gather_start(2 * s)

    last = H + 1
    relay(0, 2)
    relay(1, 1)
    step_in(0)
    for j in range(3, last + 1):
        relay(0, j)
        relay(1, j - 1)
        if j == 3:
            relay(2, 1)
        else:
            relay(2, j - 2)
    finish(0)
    gather_wait(0)
    reduce_start(0, [(0, 6)])
    relay(1, last)
    relay(2, last - 1)
    relay(3, 1)

    squares = None
    for s in range(3):
        solved = reduce_wait(2 * s)
        XG[2 * s + 1, x] = solved
        gather_start(2 * s + 1)
        squares = emit(s, solved, squares)
        if s == 0:
            relay(2, last)
            relay(3, 2)
            finish(1)
            gather_wait(1)
            reduce_start(1, [(1, 0)])
            relay(3, 3)
            relay(4, 1)
        elif s == 1:
            relay(4, 4)
            relay(5, 3)
            relay(6, 1)
            gather_wait(3)
            reduce_start(3, [(3, 2)], early=0)
            relay(4, 5)
            relay(5, 4)
            relay(6, 2)
            finish(4)
        else:
            relay(6, 5)
            gather_wait(5)
            reduce_start(5, [(5, 5)], early=1)
            finish(6)
        step_in(s + 1)
        if s == 0:
            relay(3, 4)
            relay(4, 2)
            relay(5, 1)
            finish(2)
            gather_wait(2)
            reduce_start(2, [(2, 7)])
            relay(3, 5)
            relay(4, 3)
            relay(5, 2)
            finish(3)
            early(0, [(1, 1)])
        elif s == 1:
            relay(5, 5)
            relay(6, 3)
            gather_wait(4)
            reduce_start(4, [(4, 8)])
            relay(6, 4)
            finish(5)
            early(1, [(1, 3), (3, 4)])
        else:
            gather_wait(6)
            reduce_start(6, [(6, 9)])
    solved = reduce_wait(6)
    PB[6, 0] = solved
    squares = emit(3, solved, squares)

    VB[0] = jnp.broadcast_to(squares, VB.shape[1:])
    for d in range(1, X):
        Copy(VB.at[0], VX.at[d], vx_s.at[d], vx_r.at[d], xpeer[d]).start()
    total = VB[0]
    for d in range(1, X):
        arrived(VX.at[d], vx_r.at[d])
        total = total + VX[d]
    VB[1] = total
    for yy in range(Y):
        for b in range(2):
            Copy(
                VB.at[1], VN.at[y, k], vn_s.at[yy, b], vn_r.at[y, k], o_to[yy][b], o_to_self[yy][b]
            ).start()
    for yy in range(Y):
        for c in range(2):
            arrived(VN.at[yy, c], vn_r.at[yy, c])
    for c in range(2):
        total = VN[0, c]
        for yy in range(1, Y):
            total = total + VN[yy, c]
        var_ref[:, pl.ds(c * w, w)] = prior_ref[:, pl.ds(c * w, w)] - total[0:1] / OBS
    for s in range(4):
        for c in range(2):
            arrived(out_ref.at[s, :, pl.ds(c * w, w)], out_r.at[s, c])
    for copy in pending:
        copy.wait_send()


def body(X, lower, dinv, kcols, prior):
    h, wide = kcols.shape[1], kcols.shape[2]
    q, w, Z = 2 * h, wide // 2, 2 * X
    vmem = pl.BlockSpec(memory_space=pltpu.VMEM)
    dma = pltpu.SemaphoreType.DMA
    out, var = pl.pallas_call(
        functools.partial(kernel, X),
        out_shape=(
            jax.ShapeDtypeStruct(kcols.shape, F32),
            jax.ShapeDtypeStruct((1, wide), F32),
        ),
        in_specs=[vmem] * 4,
        out_specs=(vmem, vmem),
        scratch_shapes=[
            pltpu.VMEM((10, 2, Z, h, wide), F32),
            pltpu.VMEM((10, 2, X, 2 * q, wide), BF16),
            pltpu.VMEM((7, 2, X * q // 2, 2 * w), BF16),
            pltpu.VMEM((4, 2, h, w), F32),
            pltpu.VMEM((7, X, q, w), F32),
            pltpu.VMEM((7, X, q, w), F32),
            pltpu.VMEM((7, X, q, w), F32),
            pltpu.VMEM((2, X, q, w), F32),
            pltpu.VMEM((2, 8, w), F32),
            pltpu.VMEM((X, 8, w), F32),
            pltpu.VMEM((X, 2, 8, w), F32),
            dma((7, 2, Z // 2 + 1)),
            dma((7, 2, Z // 2 + 1)),
            dma((7, 2, Z // 2 + 1)),
            dma((7, 2, Z // 2 + 1)),
            dma((4,)),
            dma((3,)),
            dma((7, X)),
            dma((7, X)),
            dma((7, X)),
            dma((7, X)),
            dma((2, 2)),
            dma((2, 2)),
            dma((4, 2)),
            dma((4, 2)),
            dma((X,)),
            dma((X,)),
            dma((X, 2)),
            dma((X, 2)),
        ],
        compiler_params=pltpu.CompilerParams(
            collective_id=0, has_side_effects=True, vmem_limit_bytes=60 * 1024 * 1024
        ),
    )(lower, dinv, kcols, prior.reshape(1, wide))
    return out, var.reshape(wide)


def solution(mesh):
    in_specs = (P(None, "row", "col"), P(None, "row", "col"), P(None, "row", "col"), P("col"))
    out_specs = (P(None, "row", "col"), P("col"))
    return jax.shard_map(
        functools.partial(body, mesh.shape["col"] // 2),
        mesh=mesh,
        in_specs=in_specs,
        out_specs=out_specs,
        check_vma=False,
    )
```

```python
import functools

import jax
import jax.numpy as jnp
from jax import lax
from jax.experimental import pallas as pl
from jax.experimental.pallas import tpu as pltpu
from jax.sharding import PartitionSpec as P

OBS = 8192
MESH = pl.DeviceIdType.MESH
F32 = jnp.float32
BF16 = jnp.bfloat16


ORDER = (6, 0, 7, 1, 2, 8, 3, 4, 5, 9)
GROUPS = tuple((b, 1) for b in ORDER)


def kernel(
    X,
    lower_ref,
    dinv_ref,
    kcols_ref,
    prior_ref,
    out_ref,
    var_ref,
    G,
    HL,
    W,
    KX,
    KB,
    XG,
    PB,
    RR,
    PE,
    OB,
    VB,
    VP,
    VZ,
    ring_s,
    ring_r,
    sib_s,
    sib_r,
    own_s,
    own_r,
    gat_s,
    gat_r,
    red_s,
    red_r,
    kx_s,
    kx_r,
    kz_s,
    kz_r,
    oz_s,
    oz_r,
    ox_s,
    ox_r,
    vp_s,
    vp_r,
    vz_s,
    vz_r,
):
    Y, Z = X, 2 * X
    H = Z // 2
    row, col = lax.axis_index("row"), lax.axis_index("col")
    y, z = row // Z, lax.rem(row, Z)
    x, k = col // 2, lax.rem(col, 2)
    h = kcols_ref.shape[1]
    t = h // X
    q = Z * t
    w = kcols_ref.shape[2] // 2

    def dev(dx, dy, dz, dk):
        return (dy * Z + dz, dx * 2 + dk)

    def up(v, d, m):
        return lax.rem(v + d, m)

    pending = []

    class Copy:
        def __init__(self, src, dst, ssem, rsem, target, me=None):
            self.me = me
            self.remote = pltpu.make_async_remote_copy(
                src_ref=src, dst_ref=dst, send_sem=ssem, recv_sem=rsem, device_id=target, device_id_type=MESH
            )
            self.local = None if me is None else pltpu.make_async_copy(src, dst, rsem)

        def start(self):
            pending.append(self)
            if self.me is None:
                self.remote.start()
            else:
                pl.when(self.me)(self.local.start)
                pl.when(jnp.logical_not(self.me))(self.remote.start)

        def wait_send(self):
            if self.me is None:
                self.remote.wait_send()
            else:
                pl.when(jnp.logical_not(self.me))(self.remote.wait_send)

    def arrived(dst, rsem):
        pltpu.make_async_copy(dst, dst, rsem).wait()

    xpeer = [None] + [dev(up(x, d, X), y, z, k) for d in range(1, X)]
    ypeer = [None] + [dev(x, up(y, d, Y), z, k) for d in range(1, Y)]
    zpeer = [None] + [dev(x, y, up(z, d, Z), k) for d in range(1, Z)]
    sibling = dev(x, y, z, 1 - k)
    far = (2, 1, 3) if X == 4 else tuple(range(1, X))

    barrier = pltpu.get_barrier_semaphore()

    def greet(target, me=None):
        def signal():
            pl.semaphore_signal(barrier, inc=1, device_id=target, device_id_type=MESH)

        if me is None:
            signal()
        else:
            pl.when(jnp.logical_not(me))(signal)

    mine = x == z // 2
    for target in zpeer[1:] + xpeer[1:] + ypeer[1:] + [sibling]:
        greet(target)
    for yy in range(Y):
        greet(dev(y, yy, z, k), (x == y) & (y == yy))
    for xx in range(X):
        for yy in range(Y):
            pl.when(mine)(functools.partial(greet, dev(xx, yy, z, k), (x == xx) & (y == yy)))
    pl.semaphore_wait(barrier, 2 * Z + 2 * X - 2 + X + Y - Z - jnp.where(x == y, 1, 0) - jnp.where(mine, 1, 0))

    def piece(g, zz, kk):
        b0, nb = GROUPS[g]
        return G.at[pl.ds(b0, nb), kk, zz]

    def spread(g):
        b0, nb = GROUPS[g]
        src = lower_ref.at[pl.ds(b0, nb)] if b0 < 6 else dinv_ref.at[pl.ds(b0 - 6, nb)]
        for xx in range(X):
            Copy(
                src.at[:, pl.ds(xx * t, t), :],
                G.at[pl.ds(b0, nb), k, z, y],
                own_s.at[g, xx],
                own_r.at[g, y],
                dev(xx, x, z, k),
                (x == xx) & (x == y),
            ).start()

    def z_send(g, d, what, lane, rows=None):
        at = up(z, what % Z, Z)
        ref = piece(g, at, k)
        if rows is not None:
            ref = ref.at[:, pl.ds(*rows)]
        Copy(ref, ref, ring_s.at[g, lane], ring_r.at[g, lane], zpeer[d % Z]).start()

    def z_arrived(g, what, lane, rows=None):
        ref = piece(g, up(z, what % Z, Z), k)
        if rows is not None:
            ref = ref.at[:, pl.ds(*rows)]
        arrived(ref, ring_r.at[g, lane])

    def sib_send(g, what):
        ref = piece(g, up(z, what % Z, Z), k)
        Copy(ref, ref, sib_s.at[g, what % Z], sib_r.at[g, what % Z], sibling).start()

    lower_half, upper_half = (0, Y // 2), (Y // 2, Y - Y // 2)

    def relay(g, j):
        if j == 1:
            b0, nb = GROUPS[g]
            for yy in range(Y):
                arrived(G.at[pl.ds(b0, nb), k, z, yy], own_r.at[g, yy])
            z_send(g, 1, 0, 0)
            z_send(g, -1, 0, 1)
            sib_send(g, 0)
        elif j <= H:
            for sign in (1, -1):
                what, lane = -sign * (j - 1), 2 * (j - 2) + (0 if sign == 1 else 1)
                z_arrived(g, what, lane)
                rows = None if j < H else (lower_half if sign == 1 else upper_half)
                z_send(g, sign, what, lane + 2, rows)
                sib_send(g, what)
        else:
            z_arrived(g, H, 2 * H - 2, lower_half)
            z_arrived(g, H, 2 * H - 1, upper_half)
            sib_send(g, H)

    STARTS = (0, 1, 3, 5, 6, 7, 8, 9, 10, 11)

    def slot(n):
        for g, first in enumerate(STARTS):
            if 1 <= n - first + 1 <= H + 1:
                relay(g, n - first + 1)

    def split(b):
        for kk in range(2):
            for j in range(Y):
                block = G[b, kk, :, j].reshape(q, 2 * w)
                hi = block.astype(BF16)
                HL[b, kk, j, pl.ds(0, q)] = hi
                HL[b, kk, j, pl.ds(q, q)] = (block - hi.astype(F32)).astype(BF16)

    def finish(g):
        for zz in range(Z):
            arrived(piece(g, up(z, zz, Z), 1 - k), sib_r.at[g, zz])
        b0, nb = GROUPS[g]
        for b in range(b0, b0 + nb):
            split(b)

    PARTS = ((0, 1), (1, 3))

    def strip(xx):
        return pl.ds(pl.multiple_of(xx * t, t), t)

    def half(zz):
        return pl.ds(pl.multiple_of(lax.rem(zz, 2) * w, w), w)

    def columns(part):
        ss = pl.ds(*PARTS[part])
        for d in far:
            Copy(
                kcols_ref.at[ss, strip(up(x, d, X))], KX.at[ss, x], kx_s.at[part, d], kx_r.at[part, d], xpeer[d]
            ).start()
        pltpu.make_async_copy(kcols_ref.at[ss, strip(x)], KX.at[ss, x], kx_r.at[part, 0]).start()

    def columns_on(part):
        ss = pl.ds(*PARTS[part])
        for d in range(X):
            arrived(KX.at[ss, up(x, X - d, X)], kx_r.at[part, d])
        for d in (4, 3, 5, 2, 6, 1, 7) if Z == 8 else range(1, Z):
            zz = up(z, d, Z)
            Copy(
                KX.at[ss, zz // 2, :, half(zz)], KB.at[ss, z], kz_s.at[part, d], kz_r.at[part, d], zpeer[d]
            ).start()
        pltpu.make_async_copy(KX.at[ss, z // 2, :, half(z)], KB.at[ss, z], kz_r.at[part, 0]).start()

    def columns_wait(part):
        ss = pl.ds(*PARTS[part])
        for d in range(Z):
            arrived(KB.at[ss, up(z, Z - d, Z)], kz_r.at[part, d])

    def gather_start(i):
        for d in far:
            Copy(XG.at[i, :, x], XG.at[i, :, x], gat_s.at[i, d], gat_r.at[i, d], xpeer[d]).start()

    def gather_wait(i):
        for d in range(1, X):
            arrived(XG.at[i, :, up(x, X - d, X)], gat_r.at[i, d])
        full = XG[i].reshape(X * q, w)
        hi = full.astype(BF16)
        lo = (full - hi.astype(F32)).astype(BF16)
        both = jnp.concatenate([hi, lo], axis=1)
        half = both.shape[0] // 2
        W[i, 0] = both[:half]
        W[i, 1] = both[half:]

    def product(i, b, j):
        res = jnp.dot(HL[b, 0, j], W[i, 0], preferred_element_type=F32)
        res += jnp.dot(HL[b, 1, j], W[i, 1], preferred_element_type=F32)
        return (res[:q, :w] + res[q:, w:]) + (res[:q, w:] + res[q:, :w])

    def reduce_start(i, blocks, early=None):
        for d in far + (0,):
            j = up(y, d, Y)
            total = None if early is None else PE[early, j]
            for src, b in blocks:
                term = product(src, b, j)
                total = term if total is None else total + term
            PB[i, d] = total
            if d:
                Copy(PB.at[i, d], RR.at[i, d], red_s.at[i, d], red_r.at[i, d], ypeer[d]).start()

    def early(slot, blocks):
        for j in range(Y):
            total = None
            for src, b in blocks:
                term = product(src, b, j)
                total = term if total is None else total + term
            PE[slot, j] = total

    def reduce_wait(i):
        total = PB[i, 0]
        for d in range(1, Y):
            arrived(RR.at[i, d], red_r.at[i, d])
            total = total + RR[i, d]
        return total

    def emit(s, solved, squares):
        src = XG.at[2 * s + 1]
        for d in (4, 3, 5, 2, 6, 1, 7) if Z == 8 else range(1, Z):
            Copy(
                src.at[up(z, d, Z), x], OB.at[s, z // 2, :, half(z)], oz_s.at[s, d], oz_r.at[s, d], zpeer[d]
            ).start()
        pltpu.make_async_copy(src.at[z, x], OB.at[s, z // 2, :, half(z)], oz_r.at[s, 0]).start()
        part = jnp.sum(solved * solved, axis=0, keepdims=True)
        return part if squares is None else squares + part

    def deliver(s):
        for d in range(Z):
            zz = up(z, Z - d, Z)
            arrived(OB.at[s, zz // 2, :, half(zz)], oz_r.at[s, d])
        for d in far:
            Copy(OB.at[s, up(x, d, X)], out_ref.at[s, strip(x)], ox_s.at[s, d], ox_r.at[s, d], xpeer[d]).start()
        pltpu.make_async_copy(OB.at[s, x], out_ref.at[s, strip(x)], ox_r.at[s, 0]).start()

    def step_in(s):
        columns = KB[s].reshape(q, w)
        if s:
            columns = columns - reduce_wait(2 * s - 1)
        XG[2 * s, :, x] = columns.reshape(Z, t, w)
        gather_start(2 * s)

    spread(0)
    columns(0)
    spread(1)
    spread(2)
    columns(1)
    for g in range(3, 10):
        spread(g)

    slot(0)
    columns_on(0)
    slot(1)
    slot(2)
    columns_wait(0)
    step_in(0)
    slot(3)
    columns_on(1)
    slot(4)
    finish(0)
    gather_wait(0)
    reduce_start(0, [(0, 6)])
    slot(5)

    squares = None
    for s in range(3):
        solved = reduce_wait(2 * s)
        XG[2 * s + 1, :, x] = solved.reshape(Z, t, w)
        gather_start(2 * s + 1)
        squares = emit(s, solved, squares)
        slot(4 * s + 6)
        if s == 0:
            finish(1)
            gather_wait(1)
            reduce_start(1, [(1, 0)])
            columns_wait(1)
        elif s == 1:
            finish(4)
            gather_wait(3)
            reduce_start(3, [(3, 2)], early=0)
        else:
            finish(7)
            early(1, [(1, 3), (3, 4)])
            finish(8)
            gather_wait(5)
            reduce_start(5, [(5, 5)], early=1)
        slot(4 * s + 7)
        deliver(s)
        step_in(s + 1)
        slot(4 * s + 8)
        if s == 0:
            finish(2)
            gather_wait(2)
            reduce_start(2, [(2, 7)])
        elif s == 1:
            finish(5)
            gather_wait(4)
            reduce_start(4, [(4, 8)])
        else:
            finish(9)
            gather_wait(6)
            reduce_start(6, [(6, 9)])
        slot(4 * s + 9)
        if s == 0:
            finish(3)
            early(0, [(1, 1)])
        elif s == 1:
            finish(6)
    solved = reduce_wait(6)
    XG[7, :, x] = solved.reshape(Z, t, w)
    squares = emit(3, solved, squares)

    VB[0] = jnp.broadcast_to(squares, VB.shape[1:])
    for yy in range(Y):
        Copy(
            VB.at[0], VP.at[x, y], vp_s.at[yy], vp_r.at[x, y], dev(z // 2, yy, z, k), mine & (y == yy)
        ).start()

    @pl.when(mine)
    def _():
        total = None
        for xx in range(X):
            for yy in range(Y):
                arrived(VP.at[xx, yy], vp_r.at[xx, yy])
                total = VP[xx, yy] if total is None else total + VP[xx, yy]
        VB[1] = total
        for d in range(1, Z):
            pltpu.make_async_remote_copy(
                src_ref=VB.at[1],
                dst_ref=VZ.at[lax.rem(z, 2)],
                send_sem=vz_s.at[d],
                recv_sem=vz_r.at[lax.rem(z, 2)],
                device_id=zpeer[d],
                device_id_type=MESH,
            ).start()
        pltpu.make_async_copy(VB.at[1], VZ.at[lax.rem(z, 2)], vz_r.at[lax.rem(z, 2)]).start()

    deliver(3)
    for c in range(2):
        arrived(VZ.at[c], vz_r.at[c])
        var_ref[:, pl.ds(c * w, w)] = prior_ref[:, pl.ds(c * w, w)] - VZ[c, 0:1] / OBS
    for s in range(4):
        for d in range(X):
            arrived(out_ref.at[s, strip(up(x, X - d, X))], ox_r.at[s, d])

    @pl.when(mine)
    def _():
        for d in range(1, Z):
            pltpu.make_async_remote_copy(
                src_ref=VB.at[1],
                dst_ref=VZ.at[lax.rem(z, 2)],
                send_sem=vz_s.at[d],
                recv_sem=vz_r.at[lax.rem(z, 2)],
                device_id=zpeer[d],
                device_id_type=MESH,
            ).wait_send()

    for copy in pending:
        copy.wait_send()


def body(X, lower, dinv, kcols, prior):
    h, wide = kcols.shape[1], kcols.shape[2]
    Z, t, w = 2 * X, h // X, wide // 2
    q = Z * t
    vmem = pl.BlockSpec(memory_space=pltpu.VMEM)
    dma = pltpu.SemaphoreType.DMA
    out, var = pl.pallas_call(
        functools.partial(kernel, X),
        out_shape=(
            jax.ShapeDtypeStruct(kcols.shape, F32),
            jax.ShapeDtypeStruct((1, wide), F32),
        ),
        in_specs=[vmem] * 4,
        out_specs=(vmem, vmem),
        scratch_shapes=[
            pltpu.VMEM((10, 2, Z, X, t, wide), F32),
            pltpu.VMEM((10, 2, X, 2 * q, wide), BF16),
            pltpu.VMEM((7, 2, X * q // 2, wide), BF16),
            pltpu.VMEM((4, X, t, wide), F32),
            pltpu.VMEM((4, Z, t, w), F32),
            pltpu.VMEM((8, Z, X, t, w), F32),
            pltpu.VMEM((7, X, q, w), F32),
            pltpu.VMEM((7, X, q, w), F32),
            pltpu.VMEM((2, X, q, w), F32),
            pltpu.VMEM((4, X, t, wide), F32),
            pltpu.VMEM((2, 8, w), F32),
            pltpu.VMEM((X, X, 8, w), F32),
            pltpu.VMEM((2, 8, w), F32),
            dma((10, 8)),
            dma((10, 8)),
            dma((10, Z)),
            dma((10, Z)),
            dma((10, X)),
            dma((10, X)),
            dma((7, X)),
            dma((7, X)),
            dma((7, X)),
            dma((7, X)),
            dma((2, X)),
            dma((2, X)),
            dma((2, Z)),
            dma((2, Z)),
            dma((4, Z)),
            dma((4, Z)),
            dma((4, X)),
            dma((4, X)),
            dma((X,)),
            dma((X, X)),
            dma((Z,)),
            dma((2,)),
        ],
        compiler_params=pltpu.CompilerParams(
            collective_id=0, has_side_effects=True, vmem_limit_bytes=60 * 1024 * 1024
        ),
    )(lower, dinv, kcols, prior.reshape(1, wide))
    return out, var.reshape(wide)


def solution(mesh):
    in_specs = (P(None, "row", "col"), P(None, "row", "col"), P(None, "row", "col"), P("col"))
    out_specs = (P(None, "row", "col"), P("col"))
    return jax.shard_map(
        functools.partial(body, mesh.shape["col"] // 2),
        mesh=mesh,
        in_specs=in_specs,
        out_specs=out_specs,
        check_vma=False,
    )
```

```python
import functools

import jax
import jax.numpy as jnp
from jax import lax
from jax.experimental import pallas as pl
from jax.experimental.pallas import tpu as pltpu
from jax.sharding import PartitionSpec as P

OBS = 8192
MESH = pl.DeviceIdType.MESH
F32 = jnp.float32
BF16 = jnp.bfloat16


ORDER = (6, 0, 7, 1, 2, 8, 3, 4, 5, 9)
GROUPS = tuple((b, 1) for b in ORDER)


def kernel(
    X,
    lower_ref,
    dinv_ref,
    kcols_ref,
    prior_ref,
    out_ref,
    var_ref,
    G,
    HL,
    W,
    KX,
    KB,
    XG,
    PB,
    RR,
    PE,
    OB,
    VB,
    VP,
    VZ,
    ring_s,
    ring_r,
    sib_s,
    sib_r,
    own_s,
    own_r,
    gat_s,
    gat_r,
    red_s,
    red_r,
    kx_s,
    kx_r,
    kz_s,
    kz_r,
    oz_s,
    oz_r,
    ox_s,
    ox_r,
    vp_s,
    vp_r,
    vz_s,
    vz_r,
):
    Y, Z = X, 2 * X
    H = Z // 2
    row, col = lax.axis_index("row"), lax.axis_index("col")
    y, z = row // Z, lax.rem(row, Z)
    x, k = col // 2, lax.rem(col, 2)
    h = kcols_ref.shape[1]
    t = h // X
    q = Z * t
    w = kcols_ref.shape[2] // 2

    def dev(dx, dy, dz, dk):
        return (dy * Z + dz, dx * 2 + dk)

    def up(v, d, m):
        return lax.rem(v + d, m)

    pending = []

    class Copy:
        def __init__(self, src, dst, ssem, rsem, target, me=None):
            self.me = me
            self.remote = pltpu.make_async_remote_copy(
                src_ref=src, dst_ref=dst, send_sem=ssem, recv_sem=rsem, device_id=target, device_id_type=MESH
            )
            self.local = None if me is None else pltpu.make_async_copy(src, dst, rsem)

        def start(self):
            pending.append(self)
            if self.me is None:
                self.remote.start()
            else:
                pl.when(self.me)(self.local.start)
                pl.when(jnp.logical_not(self.me))(self.remote.start)

        def wait_send(self):
            if self.me is None:
                self.remote.wait_send()
            else:
                pl.when(jnp.logical_not(self.me))(self.remote.wait_send)

    def arrived(dst, rsem):
        pltpu.make_async_copy(dst, dst, rsem).wait()

    xpeer = [None] + [dev(up(x, d, X), y, z, k) for d in range(1, X)]
    ypeer = [None] + [dev(x, up(y, d, Y), z, k) for d in range(1, Y)]
    zpeer = [None] + [dev(x, y, up(z, d, Z), k) for d in range(1, Z)]
    sibling = dev(x, y, z, 1 - k)
    far = (2, 1, 3) if X == 4 else tuple(range(1, X))

    barrier = pltpu.get_barrier_semaphore()

    def greet(target, me=None):
        def signal():
            pl.semaphore_signal(barrier, inc=1, device_id=target, device_id_type=MESH)

        if me is None:
            signal()
        else:
            pl.when(jnp.logical_not(me))(signal)

    mine = x == z // 2
    for target in zpeer[1:] + xpeer[1:] + ypeer[1:] + [sibling]:
        greet(target)
    for yy in range(Y):
        greet(dev(y, yy, z, k), (x == y) & (y == yy))
    for xx in range(X):
        for yy in range(Y):
            pl.when(mine)(functools.partial(greet, dev(xx, yy, z, k), (x == xx) & (y == yy)))
    pl.semaphore_wait(barrier, 2 * Z + 2 * X - 2 + X + Y - Z - jnp.where(x == y, 1, 0) - jnp.where(mine, 1, 0))

    def piece(g, zz, kk):
        b0, nb = GROUPS[g]
        return G.at[pl.ds(b0, nb), kk, zz]

    def spread(g):
        b0, nb = GROUPS[g]
        src = lower_ref.at[pl.ds(b0, nb)] if b0 < 6 else dinv_ref.at[pl.ds(b0 - 6, nb)]
        for xx in range(X):
            Copy(
                src.at[:, pl.ds(xx * t, t), :],
                G.at[pl.ds(b0, nb), k, z, y],
                own_s.at[g, xx],
                own_r.at[g, y],
                dev(xx, x, z, k),
                (x == xx) & (x == y),
            ).start()

    def z_send(g, d, what, lane, rows=None):
        at = up(z, what % Z, Z)
        ref = piece(g, at, k)
        if rows is not None:
            ref = ref.at[:, pl.ds(*rows)]
        Copy(ref, ref, ring_s.at[g, lane], ring_r.at[g, lane], zpeer[d % Z]).start()

    def z_arrived(g, what, lane, rows=None):
        ref = piece(g, up(z, what % Z, Z), k)
        if rows is not None:
            ref = ref.at[:, pl.ds(*rows)]
        arrived(ref, ring_r.at[g, lane])

    def sib_send(g, what):
        ref = piece(g, up(z, what % Z, Z), k)
        Copy(ref, ref, sib_s.at[g, what % Z], sib_r.at[g, what % Z], sibling).start()

    lower_half, upper_half = (0, Y // 2), (Y // 2, Y - Y // 2)

    def relay(g, j):
        if j == 1:
            b0, nb = GROUPS[g]
            for yy in range(Y):
                arrived(G.at[pl.ds(b0, nb), k, z, yy], own_r.at[g, yy])
            z_send(g, 1, 0, 0)
            z_send(g, -1, 0, 1)
            sib_send(g, 0)
        elif j <= H:
            for sign in (1, -1):
                what, lane = -sign * (j - 1), 2 * (j - 2) + (0 if sign == 1 else 1)
                z_arrived(g, what, lane)
                rows = None if j < H else (lower_half if sign == 1 else upper_half)
                z_send(g, sign, what, lane + 2, rows)
                sib_send(g, what)
        else:
            z_arrived(g, H, 2 * H - 2, lower_half)
            z_arrived(g, H, 2 * H - 1, upper_half)
            sib_send(g, H)

    STARTS = (0, 1, 3, 5, 6, 8, 9, 10, 10, 12)

    def slot(n):
        for g, first in enumerate(STARTS):
            if 1 <= n - first + 1 <= H + 1:
                relay(g, n - first + 1)

    def split(b):
        for kk in range(2):
            for f in range(2):
                for j in range(Y):
                    block = G[b, kk, pl.ds(f * H, H), j].reshape(q // 2, 2 * w)
                    hi = block.astype(BF16)
                    HL[b, kk, f, j, pl.ds(0, q // 2)] = hi
                    HL[b, kk, f, j, pl.ds(q // 2, q // 2)] = (block - hi.astype(F32)).astype(BF16)

    def finish(g):
        for zz in range(Z):
            arrived(piece(g, up(z, zz, Z), 1 - k), sib_r.at[g, zz])
        b0, nb = GROUPS[g]
        for b in range(b0, b0 + nb):
            split(b)

    PARTS = ((0, 1), (1, 3))

    def strip(xx):
        return pl.ds(pl.multiple_of(xx * t, t), t)

    def half(zz):
        return pl.ds(pl.multiple_of(lax.rem(zz, 2) * w, w), w)

    def columns(part):
        ss = pl.ds(*PARTS[part])
        for d in far:
            Copy(
                kcols_ref.at[ss, strip(up(x, d, X))], KX.at[ss, x], kx_s.at[part, d], kx_r.at[part, d], xpeer[d]
            ).start()
        pltpu.make_async_copy(kcols_ref.at[ss, strip(x)], KX.at[ss, x], kx_r.at[part, 0]).start()

    def columns_on(part):
        ss = pl.ds(*PARTS[part])
        for d in range(X):
            arrived(KX.at[ss, up(x, X - d, X)], kx_r.at[part, d])
        for d in (4, 3, 5, 2, 6, 1, 7) if Z == 8 else range(1, Z):
            zz = up(z, d, Z)
            Copy(
                KX.at[ss, zz // 2, :, half(zz)], KB.at[ss, z], kz_s.at[part, d], kz_r.at[part, d], zpeer[d]
            ).start()
        pltpu.make_async_copy(KX.at[ss, z // 2, :, half(z)], KB.at[ss, z], kz_r.at[part, 0]).start()

    def columns_wait(part):
        ss = pl.ds(*PARTS[part])
        for d in range(Z):
            arrived(KB.at[ss, up(z, Z - d, Z)], kz_r.at[part, d])

    def gather_start(i, f):
        ref = XG.at[i, pl.ds(f * H, H), x]
        for d in far:
            Copy(ref, ref, gat_s.at[i, f, d], gat_r.at[i, f, d], xpeer[d]).start()

    def gather_wait(i):
        for f in range(2):
            for d in range(1, X):
                arrived(XG.at[i, pl.ds(f * H, H), up(x, X - d, X)], gat_r.at[i, f, d])
            full = XG[i, pl.ds(f * H, H)].reshape(X * q // 2, w)
            hi = full.astype(BF16)
            lo = (full - hi.astype(F32)).astype(BF16)
            W[i, f] = jnp.concatenate([hi, lo], axis=1)

    def product(i, b, f, j):
        p = q // 2
        res = jnp.dot(HL[b, 0, f, j], W[i, 0], preferred_element_type=F32)
        res += jnp.dot(HL[b, 1, f, j], W[i, 1], preferred_element_type=F32)
        return (res[:p, :w] + res[p:, w:]) + (res[:p, w:] + res[p:, :w])

    def products(blocks, f, j, total=None):
        for src, b in blocks:
            term = product(src, b, f, j)
            total = term if total is None else total + term
        return total

    def reduce_start(i, blocks, early=None):
        for f in range(2):
            for d in far:
                j = up(y, d, Y)
                PB[i, f, d] = products(blocks, f, j, None if early is None else PE[early, f, j])
                Copy(PB.at[i, f, d], RR.at[i, f, d], red_s.at[i, f, d], red_r.at[i, f, d], ypeer[d]).start()
        for f in range(2):
            PB[i, f, 0] = products(blocks, f, y, None if early is None else PE[early, f, y])

    def early(slot, blocks):
        for f in range(2):
            for j in range(Y):
                PE[slot, f, j] = products(blocks, f, j)

    def reduce_wait(i, f):
        total = PB[i, f, 0]
        for d in range(1, Y):
            arrived(RR.at[i, f, d], red_r.at[i, f, d])
            total = total + RR[i, f, d]
        return total

    def emit(s):
        src = XG.at[2 * s + 1]
        for d in (4, 3, 5, 2, 6, 1, 7) if Z == 8 else range(1, Z):
            Copy(
                src.at[up(z, d, Z), x], OB.at[s, z // 2, :, half(z)], oz_s.at[s, d], oz_r.at[s, d], zpeer[d]
            ).start()
        pltpu.make_async_copy(src.at[z, x], OB.at[s, z // 2, :, half(z)], oz_r.at[s, 0]).start()

    def deliver(s):
        for d in range(Z):
            zz = up(z, Z - d, Z)
            arrived(OB.at[s, zz // 2, :, half(zz)], oz_r.at[s, d])
        for d in far:
            Copy(OB.at[s, up(x, d, X)], out_ref.at[s, strip(x)], ox_s.at[s, d], ox_r.at[s, d], xpeer[d]).start()
        pltpu.make_async_copy(OB.at[s, x], out_ref.at[s, strip(x)], ox_r.at[s, 0]).start()

    def step_in(s):
        for f in range(2):
            columns = KB[s, pl.ds(f * H, H)].reshape(q // 2, w)
            if s:
                columns = columns - reduce_wait(2 * s - 1, f)
            XG[2 * s, pl.ds(f * H, H), x] = columns.reshape(H, t, w)
            gather_start(2 * s, f)

    def step_out(s, squares):
        for f in range(2):
            solved = reduce_wait(2 * s, f)
            XG[2 * s + 1, pl.ds(f * H, H), x] = solved.reshape(H, t, w)
            if s < 3:
                gather_start(2 * s + 1, f)
            part = jnp.sum(solved * solved, axis=0, keepdims=True)
            squares = part if squares is None else squares + part
        emit(s)
        return squares

    spread(0)
    columns(0)
    spread(1)
    spread(2)
    columns(1)
    for g in range(3, 10):
        spread(g)

    slot(0)
    columns_on(0)
    slot(1)
    slot(2)
    columns_wait(0)
    step_in(0)
    slot(3)
    columns_on(1)
    slot(4)
    finish(0)
    gather_wait(0)
    reduce_start(0, [(0, 6)])
    slot(5)

    squares = None
    for s in range(3):
        squares = step_out(s, squares)
        slot(4 * s + 6)
        if s == 0:
            finish(1)
            gather_wait(1)
            reduce_start(1, [(1, 0)])
            columns_wait(1)
        elif s == 1:
            finish(4)
            gather_wait(3)
            reduce_start(3, [(3, 2)], early=0)
        else:
            finish(7)
            early(1, [(1, 3), (3, 4)])
            finish(8)
            gather_wait(5)
            reduce_start(5, [(5, 5)], early=1)
        slot(4 * s + 7)
        deliver(s)
        step_in(s + 1)
        slot(4 * s + 8)
        if s == 0:
            finish(2)
            gather_wait(2)
            reduce_start(2, [(2, 7)])
        elif s == 1:
            finish(5)
            gather_wait(4)
            reduce_start(4, [(4, 8)])
        else:
            finish(9)
            gather_wait(6)
            reduce_start(6, [(6, 9)])
        slot(4 * s + 9)
        if s == 0:
            finish(3)
            early(0, [(1, 1)])
        elif s == 1:
            finish(6)
    squares = step_out(3, squares)

    VB[0] = jnp.broadcast_to(squares, VB.shape[1:])
    for yy in range(Y):
        Copy(
            VB.at[0], VP.at[x, y], vp_s.at[yy], vp_r.at[x, y], dev(z // 2, yy, z, k), mine & (y == yy)
        ).start()

    @pl.when(mine)
    def _():
        total = None
        for xx in range(X):
            for yy in range(Y):
                arrived(VP.at[xx, yy], vp_r.at[xx, yy])
                total = VP[xx, yy] if total is None else total + VP[xx, yy]
        VB[1] = total
        for d in range(1, Z):
            pltpu.make_async_remote_copy(
                src_ref=VB.at[1],
                dst_ref=VZ.at[lax.rem(z, 2)],
                send_sem=vz_s.at[d],
                recv_sem=vz_r.at[lax.rem(z, 2)],
                device_id=zpeer[d],
                device_id_type=MESH,
            ).start()
        pltpu.make_async_copy(VB.at[1], VZ.at[lax.rem(z, 2)], vz_r.at[lax.rem(z, 2)]).start()

    deliver(3)
    for c in range(2):
        arrived(VZ.at[c], vz_r.at[c])
        var_ref[:, pl.ds(c * w, w)] = prior_ref[:, pl.ds(c * w, w)] - VZ[c, 0:1] / OBS
    for s in range(4):
        for d in range(X):
            arrived(out_ref.at[s, strip(up(x, X - d, X))], ox_r.at[s, d])

    @pl.when(mine)
    def _():
        for d in range(1, Z):
            pltpu.make_async_remote_copy(
                src_ref=VB.at[1],
                dst_ref=VZ.at[lax.rem(z, 2)],
                send_sem=vz_s.at[d],
                recv_sem=vz_r.at[lax.rem(z, 2)],
                device_id=zpeer[d],
                device_id_type=MESH,
            ).wait_send()

    for copy in pending:
        copy.wait_send()


def body(X, lower, dinv, kcols, prior):
    h, wide = kcols.shape[1], kcols.shape[2]
    Z, t, w = 2 * X, h // X, wide // 2
    q = Z * t
    vmem = pl.BlockSpec(memory_space=pltpu.VMEM)
    dma = pltpu.SemaphoreType.DMA
    out, var = pl.pallas_call(
        functools.partial(kernel, X),
        out_shape=(
            jax.ShapeDtypeStruct(kcols.shape, F32),
            jax.ShapeDtypeStruct((1, wide), F32),
        ),
        in_specs=[vmem] * 4,
        out_specs=(vmem, vmem),
        scratch_shapes=[
            pltpu.VMEM((10, 2, Z, X, t, wide), F32),
            pltpu.VMEM((10, 2, 2, X, q, wide), BF16),
            pltpu.VMEM((7, 2, X * q // 2, wide), BF16),
            pltpu.VMEM((4, X, t, wide), F32),
            pltpu.VMEM((4, Z, t, w), F32),
            pltpu.VMEM((8, Z, X, t, w), F32),
            pltpu.VMEM((7, 2, X, q // 2, w), F32),
            pltpu.VMEM((7, 2, X, q // 2, w), F32),
            pltpu.VMEM((2, 2, X, q // 2, w), F32),
            pltpu.VMEM((4, X, t, wide), F32),
            pltpu.VMEM((2, 8, w), F32),
            pltpu.VMEM((X, X, 8, w), F32),
            pltpu.VMEM((2, 8, w), F32),
            dma((10, 8)),
            dma((10, 8)),
            dma((10, Z)),
            dma((10, Z)),
            dma((10, X)),
            dma((10, X)),
            dma((7, 2, X)),
            dma((7, 2, X)),
            dma((7, 2, X)),
            dma((7, 2, X)),
            dma((2, X)),
            dma((2, X)),
            dma((2, Z)),
            dma((2, Z)),
            dma((4, Z)),
            dma((4, Z)),
            dma((4, X)),
            dma((4, X)),
            dma((X,)),
            dma((X, X)),
            dma((Z,)),
            dma((2,)),
        ],
        compiler_params=pltpu.CompilerParams(
            collective_id=0, has_side_effects=True, vmem_limit_bytes=60 * 1024 * 1024
        ),
    )(lower, dinv, kcols, prior.reshape(1, wide))
    return out, var.reshape(wide)


def solution(mesh):
    in_specs = (P(None, "row", "col"), P(None, "row", "col"), P(None, "row", "col"), P("col"))
    out_specs = (P(None, "row", "col"), P("col"))
    return jax.shard_map(
        functools.partial(body, mesh.shape["col"] // 2),
        mesh=mesh,
        in_specs=in_specs,
        out_specs=out_specs,
        check_vma=False,
    )
```

```python
import functools

import jax
import jax.numpy as jnp
from jax import lax
from jax.experimental import pallas as pl
from jax.experimental.pallas import tpu as pltpu
from jax.sharding import PartitionSpec as P

OBS = 8192
MESH = pl.DeviceIdType.MESH
F32 = jnp.float32
BF16 = jnp.bfloat16


ORDER = (6, 0, 7, 1, 2, 8, 3, 4, 5, 9)
GROUPS = tuple((b, 1) for b in ORDER)


def kernel(
    X,
    lower_ref,
    dinv_ref,
    kcols_ref,
    prior_ref,
    out_ref,
    var_ref,
    G,
    HL,
    W,
    KX,
    KB,
    XG,
    PB,
    RR,
    PE,
    OB,
    VB,
    VP,
    VZ,
    ring_s,
    ring_r,
    sib_s,
    sib_r,
    own_s,
    own_r,
    gat_s,
    gat_r,
    red_s,
    red_r,
    kx_s,
    kx_r,
    kz_s,
    kz_r,
    oz_s,
    oz_r,
    ox_s,
    ox_r,
    vp_s,
    vp_r,
    vz_s,
    vz_r,
):
    Y, Z = X, 2 * X
    H = Z // 2
    row, col = lax.axis_index("row"), lax.axis_index("col")
    y, z = row // Z, lax.rem(row, Z)
    x, k = col // 2, lax.rem(col, 2)
    h = kcols_ref.shape[1]
    t = h // X
    q = Z * t
    w = kcols_ref.shape[2] // 2

    def dev(dx, dy, dz, dk):
        return (dy * Z + dz, dx * 2 + dk)

    def up(v, d, m):
        return lax.rem(v + d, m)

    pending = []

    class Copy:
        def __init__(self, src, dst, ssem, rsem, target, me=None):
            self.me = me
            self.remote = pltpu.make_async_remote_copy(
                src_ref=src, dst_ref=dst, send_sem=ssem, recv_sem=rsem, device_id=target, device_id_type=MESH
            )
            self.local = None if me is None else pltpu.make_async_copy(src, dst, rsem)

        def start(self):
            pending.append(self)
            if self.me is None:
                self.remote.start()
            else:
                pl.when(self.me)(self.local.start)
                pl.when(jnp.logical_not(self.me))(self.remote.start)

        def wait_send(self):
            if self.me is None:
                self.remote.wait_send()
            else:
                pl.when(jnp.logical_not(self.me))(self.remote.wait_send)

    def arrived(dst, rsem):
        pltpu.make_async_copy(dst, dst, rsem).wait()

    xpeer = [None] + [dev(up(x, d, X), y, z, k) for d in range(1, X)]
    ypeer = [None] + [dev(x, up(y, d, Y), z, k) for d in range(1, Y)]
    zpeer = [None] + [dev(x, y, up(z, d, Z), k) for d in range(1, Z)]
    sibling = dev(x, y, z, 1 - k)
    far = (2, 1, 3) if X == 4 else tuple(range(1, X))

    barrier = pltpu.get_barrier_semaphore()

    def greet(target, me=None):
        def signal():
            pl.semaphore_signal(barrier, inc=1, device_id=target, device_id_type=MESH)

        if me is None:
            signal()
        else:
            pl.when(jnp.logical_not(me))(signal)

    mine = x == z // 2
    for target in zpeer[1:] + xpeer[1:] + ypeer[1:] + [sibling]:
        greet(target)
    for yy in range(Y):
        greet(dev(y, yy, z, k), (x == y) & (y == yy))
    for xx in range(X):
        for yy in range(Y):
            pl.when(mine)(functools.partial(greet, dev(xx, yy, z, k), (x == xx) & (y == yy)))
    pl.semaphore_wait(barrier, 2 * Z + 2 * X - 2 + X + Y - Z - jnp.where(x == y, 1, 0) - jnp.where(mine, 1, 0))

    def piece(g, zz, kk):
        b0, nb = GROUPS[g]
        return G.at[pl.ds(b0, nb), kk, zz]

    def spread(g):
        b0, nb = GROUPS[g]
        src = lower_ref.at[pl.ds(b0, nb)] if b0 < 6 else dinv_ref.at[pl.ds(b0 - 6, nb)]
        for xx in range(X):
            Copy(
                src.at[:, pl.ds(xx * t, t), :],
                G.at[pl.ds(b0, nb), k, z, y],
                own_s.at[g, xx],
                own_r.at[g, y],
                dev(xx, x, z, k),
                (x == xx) & (x == y),
            ).start()

    def z_send(g, d, what, lane, rows=None):
        at = up(z, what % Z, Z)
        ref = piece(g, at, k)
        if rows is not None:
            ref = ref.at[:, pl.ds(*rows)]
        Copy(ref, ref, ring_s.at[g, lane], ring_r.at[g, lane], zpeer[d % Z]).start()

    def z_arrived(g, what, lane, rows=None):
        ref = piece(g, up(z, what % Z, Z), k)
        if rows is not None:
            ref = ref.at[:, pl.ds(*rows)]
        arrived(ref, ring_r.at[g, lane])

    def sib_send(g, what):
        ref = piece(g, up(z, what % Z, Z), k)
        Copy(ref, ref, sib_s.at[g, what % Z], sib_r.at[g, what % Z], sibling).start()

    lower_half, upper_half = (0, Y // 2), (Y // 2, Y - Y // 2)

    def relay(g, j):
        if j == 1:
            b0, nb = GROUPS[g]
            for yy in range(Y):
                arrived(G.at[pl.ds(b0, nb), k, z, yy], own_r.at[g, yy])
            z_send(g, 1, 0, 0)
            z_send(g, -1, 0, 1)
            sib_send(g, 0)
        elif j <= H:
            for sign in (1, -1):
                what, lane = -sign * (j - 1), 2 * (j - 2) + (0 if sign == 1 else 1)
                z_arrived(g, what, lane)
                rows = None if j < H else (lower_half if sign == 1 else upper_half)
                z_send(g, sign, what, lane + 2, rows)
                sib_send(g, what)
        else:
            z_arrived(g, H, 2 * H - 2, lower_half)
            z_arrived(g, H, 2 * H - 1, upper_half)
            sib_send(g, H)

    STARTS = (0, 1, 3, 5, 6, 8, 9, 10, 10, 12)

    def slot(n):
        for g, first in enumerate(STARTS):
            if 1 <= n - first + 1 <= H + 1:
                relay(g, n - first + 1)

    def split(b):
        for kk in range(2):
            for j in range(Y):
                block = G[b, kk, :, j].reshape(q, 2 * w)
                hi = block.astype(BF16)
                HL[b, kk, j, pl.ds(0, q)] = hi
                HL[b, kk, j, pl.ds(q, q)] = (block - hi.astype(F32)).astype(BF16)

    def finish(g):
        for zz in range(Z):
            arrived(piece(g, up(z, zz, Z), 1 - k), sib_r.at[g, zz])
        b0, nb = GROUPS[g]
        for b in range(b0, b0 + nb):
            split(b)

    PARTS = ((0, 1), (1, 3))

    def strip(xx):
        return pl.ds(pl.multiple_of(xx * t, t), t)

    def half(zz):
        return pl.ds(pl.multiple_of(lax.rem(zz, 2) * w, w), w)

    def columns(part):
        ss = pl.ds(*PARTS[part])
        for d in far:
            Copy(
                kcols_ref.at[ss, strip(up(x, d, X))], KX.at[ss, x], kx_s.at[part, d], kx_r.at[part, d], xpeer[d]
            ).start()
        pltpu.make_async_copy(kcols_ref.at[ss, strip(x)], KX.at[ss, x], kx_r.at[part, 0]).start()

    def columns_on(part):
        ss = pl.ds(*PARTS[part])
        for d in range(X):
            arrived(KX.at[ss, up(x, X - d, X)], kx_r.at[part, d])
        for d in (4, 3, 5, 2, 6, 1, 7) if Z == 8 else range(1, Z):
            zz = up(z, d, Z)
            Copy(
                KX.at[ss, zz // 2, :, half(zz)], KB.at[ss, z], kz_s.at[part, d], kz_r.at[part, d], zpeer[d]
            ).start()
        pltpu.make_async_copy(KX.at[ss, z // 2, :, half(z)], KB.at[ss, z], kz_r.at[part, 0]).start()

    def columns_wait(part):
        ss = pl.ds(*PARTS[part])
        for d in range(Z):
            arrived(KB.at[ss, up(z, Z - d, Z)], kz_r.at[part, d])

    def gather_start(i):
        for d in far:
            Copy(XG.at[i, :, x], XG.at[i, :, x], gat_s.at[i, d], gat_r.at[i, d], xpeer[d]).start()

    def gather_wait(i):
        for d in range(1, X):
            arrived(XG.at[i, :, up(x, X - d, X)], gat_r.at[i, d])
        full = XG[i].reshape(X * q, w)
        hi = full.astype(BF16)
        lo = (full - hi.astype(F32)).astype(BF16)
        both = jnp.concatenate([hi, lo], axis=1)
        half = both.shape[0] // 2
        W[i, 0] = both[:half]
        W[i, 1] = both[half:]

    def product(i, b, j):
        res = jnp.dot(HL[b, 0, j], W[i, 0], preferred_element_type=F32)
        res += jnp.dot(HL[b, 1, j], W[i, 1], preferred_element_type=F32)
        return (res[:q, :w] + res[q:, w:]) + (res[:q, w:] + res[q:, :w])

    def reduce_start(i, blocks, early=None):
        for d in far + (0,):
            j = up(y, d, Y)
            total = None if early is None else PE[early, j]
            for src, b in blocks:
                term = product(src, b, j)
                total = term if total is None else total + term
            PB[i, d] = total
            if d:
                Copy(PB.at[i, d], RR.at[i, d], red_s.at[i, d], red_r.at[i, d], ypeer[d]).start()

    def early(slot, blocks):
        for j in range(Y):
            total = None
            for src, b in blocks:
                term = product(src, b, j)
                total = term if total is None else total + term
            PE[slot, j] = total

    def reduce_wait(i):
        total = PB[i, 0]
        for d in range(1, Y):
            arrived(RR.at[i, d], red_r.at[i, d])
            total = total + RR[i, d]
        return total

    def emit(s, solved, squares):
        src = XG.at[2 * s + 1]
        for d in (4, 3, 5, 2, 6, 1, 7) if Z == 8 else range(1, Z):
            Copy(
                src.at[up(z, d, Z), x], OB.at[s, z // 2, :, half(z)], oz_s.at[s, d], oz_r.at[s, d], zpeer[d]
            ).start()
        pltpu.make_async_copy(src.at[z, x], OB.at[s, z // 2, :, half(z)], oz_r.at[s, 0]).start()
        part = jnp.sum(solved * solved, axis=0, keepdims=True)
        return part if squares is None else squares + part

    def deliver(s):
        for d in range(Z):
            zz = up(z, Z - d, Z)
            arrived(OB.at[s, zz // 2, :, half(zz)], oz_r.at[s, d])
        for d in far:
            Copy(OB.at[s, up(x, d, X)], out_ref.at[s, strip(x)], ox_s.at[s, d], ox_r.at[s, d], xpeer[d]).start()
        pltpu.make_async_copy(OB.at[s, x], out_ref.at[s, strip(x)], ox_r.at[s, 0]).start()

    def step_in(s):
        columns = KB[s].reshape(q, w)
        if s:
            columns = columns - reduce_wait(2 * s - 1)
        XG[2 * s, :, x] = columns.reshape(Z, t, w)
        gather_start(2 * s)

    spread(0)
    columns(0)
    spread(1)
    spread(2)
    columns(1)
    for g in range(3, 10):
        spread(g)

    slot(0)
    columns_on(0)
    slot(1)
    slot(2)
    columns_wait(0)
    step_in(0)
    slot(3)
    columns_on(1)
    slot(4)
    finish(0)
    gather_wait(0)
    reduce_start(0, [(0, 6)])
    slot(5)

    squares = None
    for s in range(3):
        solved = reduce_wait(2 * s)
        XG[2 * s + 1, :, x] = solved.reshape(Z, t, w)
        gather_start(2 * s + 1)
        squares = emit(s, solved, squares)
        slot(4 * s + 6)
        if s == 0:
            finish(1)
            gather_wait(1)
            reduce_start(1, [(1, 0)])
            columns_wait(1)
        elif s == 1:
            finish(4)
            gather_wait(3)
            reduce_start(3, [(3, 2)], early=0)
        else:
            finish(7)
            early(1, [(1, 3), (3, 4)])
            finish(8)
            gather_wait(5)
            reduce_start(5, [(5, 5)], early=1)
        slot(4 * s + 7)
        deliver(s)
        step_in(s + 1)
        slot(4 * s + 8)
        if s == 0:
            finish(2)
            gather_wait(2)
            reduce_start(2, [(2, 7)])
        elif s == 1:
            finish(5)
            gather_wait(4)
            reduce_start(4, [(4, 8)])
        else:
            finish(9)
            gather_wait(6)
            reduce_start(6, [(6, 9)])
        slot(4 * s + 9)
        if s == 0:
            finish(3)
            early(0, [(1, 1)])
        elif s == 1:
            finish(6)
    solved = reduce_wait(6)
    XG[7, :, x] = solved.reshape(Z, t, w)
    squares = emit(3, solved, squares)

    VB[0] = jnp.broadcast_to(squares, VB.shape[1:])
    for yy in range(Y):
        Copy(
            VB.at[0], VP.at[x, y], vp_s.at[yy], vp_r.at[x, y], dev(z // 2, yy, z, k), mine & (y == yy)
        ).start()

    @pl.when(mine)
    def _():
        total = None
        for xx in range(X):
            for yy in range(Y):
                arrived(VP.at[xx, yy], vp_r.at[xx, yy])
                total = VP[xx, yy] if total is None else total + VP[xx, yy]
        VB[1] = total
        for d in range(1, Z):
            pltpu.make_async_remote_copy(
                src_ref=VB.at[1],
                dst_ref=VZ.at[lax.rem(z, 2)],
                send_sem=vz_s.at[d],
                recv_sem=vz_r.at[lax.rem(z, 2)],
                device_id=zpeer[d],
                device_id_type=MESH,
            ).start()
        pltpu.make_async_copy(VB.at[1], VZ.at[lax.rem(z, 2)], vz_r.at[lax.rem(z, 2)]).start()

    deliver(3)
    for c in range(2):
        arrived(VZ.at[c], vz_r.at[c])
        var_ref[:, pl.ds(c * w, w)] = prior_ref[:, pl.ds(c * w, w)] - VZ[c, 0:1] / OBS
    for s in range(4):
        for d in range(X):
            arrived(out_ref.at[s, strip(up(x, X - d, X))], ox_r.at[s, d])

    @pl.when(mine)
    def _():
        for d in range(1, Z):
            pltpu.make_async_remote_copy(
                src_ref=VB.at[1],
                dst_ref=VZ.at[lax.rem(z, 2)],
                send_sem=vz_s.at[d],
                recv_sem=vz_r.at[lax.rem(z, 2)],
                device_id=zpeer[d],
                device_id_type=MESH,
            ).wait_send()

    for copy in pending:
        copy.wait_send()


def body(X, lower, dinv, kcols, prior):
    h, wide = kcols.shape[1], kcols.shape[2]
    Z, t, w = 2 * X, h // X, wide // 2
    q = Z * t
    vmem = pl.BlockSpec(memory_space=pltpu.VMEM)
    dma = pltpu.SemaphoreType.DMA
    out, var = pl.pallas_call(
        functools.partial(kernel, X),
        out_shape=(
            jax.ShapeDtypeStruct(kcols.shape, F32),
            jax.ShapeDtypeStruct((1, wide), F32),
        ),
        in_specs=[vmem] * 4,
        out_specs=(vmem, vmem),
        scratch_shapes=[
            pltpu.VMEM((10, 2, Z, X, t, wide), F32),
            pltpu.VMEM((10, 2, X, 2 * q, wide), BF16),
            pltpu.VMEM((7, 2, X * q // 2, wide), BF16),
            pltpu.VMEM((4, X, t, wide), F32),
            pltpu.VMEM((4, Z, t, w), F32),
            pltpu.VMEM((8, Z, X, t, w), F32),
            pltpu.VMEM((7, X, q, w), F32),
            pltpu.VMEM((7, X, q, w), F32),
            pltpu.VMEM((2, X, q, w), F32),
            pltpu.VMEM((4, X, t, wide), F32),
            pltpu.VMEM((2, 8, w), F32),
            pltpu.VMEM((X, X, 8, w), F32),
            pltpu.VMEM((2, 8, w), F32),
            dma((10, 8)),
            dma((10, 8)),
            dma((10, Z)),
            dma((10, Z)),
            dma((10, X)),
            dma((10, X)),
            dma((7, X)),
            dma((7, X)),
            dma((7, X)),
            dma((7, X)),
            dma((2, X)),
            dma((2, X)),
            dma((2, Z)),
            dma((2, Z)),
            dma((4, Z)),
            dma((4, Z)),
            dma((4, X)),
            dma((4, X)),
            dma((X,)),
            dma((X, X)),
            dma((Z,)),
            dma((2,)),
        ],
        compiler_params=pltpu.CompilerParams(
            collective_id=0, has_side_effects=True, vmem_limit_bytes=60 * 1024 * 1024
        ),
    )(lower, dinv, kcols, prior.reshape(1, wide))
    return out, var.reshape(wide)


def solution(mesh):
    in_specs = (P(None, "row", "col"), P(None, "row", "col"), P(None, "row", "col"), P("col"))
    out_specs = (P(None, "row", "col"), P("col"))
    return jax.shard_map(
        functools.partial(body, mesh.shape["col"] // 2),
        mesh=mesh,
        in_specs=in_specs,
        out_specs=out_specs,
        check_vma=False,
    )
```
